32 devices in a mesh: days: 8 (over z, y), cols: 4 (over x, core).
Axes of the slice: x: 2, y: 2, z: 4, core: 2. Of those that a mesh axis runs over, the one named last changes fastest.
Arguments:
- stations: int32 [64, 8], replicated, may hold values from 0 to 31, as said below
- counts: int32 [64], replicated, may hold values from 4 to 8, as said below
- q_cols: bfloat16 [4096, 4096], P(None, ('days', 'cols')), may hold values from -6 to 6, as said below
- glob_solution: float32 [4096], P(('days', 'cols')), may hold values from -6 to 6
- inv_blocks: bfloat16 [64, 4096, 128], P('days', 'cols')
- coupling: bfloat16 [64, 4096, 1024], P('days', 'cols'), may hold values from -0.1875 to 0.1875
- local_rhs: float32 [64, 4096], P('days', 'cols'), may hold values from -6 to 6
Outputs:
- local_solution: float32 [64, 4096], P('days', 'cols')
- cov_diag: float32 [64, 4096], P('days', 'cols')
The draws below stay inside these ranges and needn't reach their ends.
Inputs may be any that keep to these rules, and one draw needn't show every extreme that they name: `stations`: each day names 8 different blocks, the first counts of them observed; the days of one index of days name one block at most 2 times, and some observed block exactly 2 times. `counts`: the first day of every index of days observes 8 blocks. q_cols equals its transpose exactly.
All inputs are finite; a program needn't handle non-finite values.
Results may differ from the reference program's by a relative error of at most 0.0035.
Values may be sent and summed in bfloat16 or wider, within the bound.
A program may use at most 192 MiB of HBM per device.

```python
import jax
import jax.numpy as jnp
from jax import lax

BW = 128
KMAX = 8
L = 4096
DAY_DEV = 8
NB = 32
GP = 4096
DAYS = 64
M = 1024


def draw_stations(key, part):
    shards = DAYS // DAY_DEV
    keys = jax.random.split(key, shards)
    perms = jax.vmap(lambda single: jax.random.permutation(single, NB))(keys)
    positions = jnp.arange(DAY_DEV * KMAX) % NB
    return perms[:, positions].reshape(DAYS, KMAX).astype(jnp.int32)


def draw_counts(key, part):
    drawn = jax.random.randint(key, (DAYS,), KMAX // 2, KMAX + 1)
    first = jnp.arange(DAYS) % DAY_DEV == 0
    return jnp.where(first, KMAX, drawn).astype(jnp.int32)


def draw_q_cols(key, part):
    rows_i = jnp.arange(GP)[:, None]
    cols_j = jnp.arange(GP)[None, :]
    upper = rows_i <= cols_j
    noise = jnp.clip(jax.random.normal(jax.random.fold_in(key, 23), (GP, GP), jnp.float32), -6.0, 6.0)
    return jnp.where(upper, noise, noise.T).astype(jnp.bfloat16)


def draw_inv_blocks(key, part):
    groups = L // BW
    noise = jax.random.normal(jax.random.fold_in(key, 11), (DAYS, groups, BW, BW), jnp.float32) * (0.5 / BW ** 0.5)
    sym = 0.5 * (noise + jnp.swapaxes(noise, 2, 3))
    diag = jax.random.uniform(jax.random.fold_in(key, 12), (DAYS, groups, BW), jnp.float32, 1.0, 2.0)
    eye = jnp.eye(BW, dtype=jnp.float32)
    blocks = sym + diag[..., :, None] * eye
    return blocks.reshape(DAYS, L, BW).astype(jnp.bfloat16)


def steps_of(stream_key, dims, cuts, low, top_value):
    level = 1.0
    for position, blocks in cuts:
        draws = jax.random.uniform(jax.random.fold_in(jax.random.fold_in(stream_key, 6), position), (blocks,), jnp.float32, low / len(cuts), top_value / len(cuts))
        level = level * jnp.repeat(jnp.exp(draws), dims[position] // blocks).reshape((-1,) + (1,) * (len(dims) - 1 - position))
    return level


def normal_values(stream_key, dims, width, bound, cuts=(), kind=jnp.bfloat16):
    result = jax.random.normal(stream_key, dims, jnp.float32) * width
    if len(cuts) > 0:
        result = steps_of(stream_key, dims, cuts, -0.22, 0.18) * result
    return jnp.clip(result, min=-bound, max=bound).astype(kind)


def setup_inputs(seed: int = 0) -> dict:
    seeds = jax.random.split(jax.random.key(seed), 8)
    return {
        "stations": draw_stations(jax.random.fold_in(seeds[7], 71), 0),
        "counts": draw_counts(jax.random.fold_in(seeds[7], 71), 0),
        "q_cols": draw_q_cols(jax.random.fold_in(seeds[7], 71), 0),
        "glob_solution": normal_values(seeds[3], (GP,), 1.0, 6.0, ((0, 32),), jnp.float32),
        "inv_blocks": draw_inv_blocks(jax.random.fold_in(seeds[7], 71), 0),
        "coupling": normal_values(seeds[5], (DAYS, L, M), M ** -0.5, 0.1875, ((0, 8), (1, 4))),
        "local_rhs": normal_values(seeds[6], (DAYS, L), 1.0, 6.0, ((0, 8), (1, 4)), jnp.float32),
    }


def one_day(q_cols, glob_solution, inputs):
    station_row, count, inv_day, coup_day, rhs_day = inputs
    groups = L // BW
    valid = (jnp.arange(KMAX) < count).astype(jnp.float32)
    colmask = jnp.repeat(valid, BW)
    index = (station_row[:, None] * BW + jnp.arange(BW)[None, :]).reshape(M).astype(jnp.int32)
    x_sel = (glob_solution[index] * colmask).astype(jnp.bfloat16)
    resid = (rhs_day - jnp.dot(coup_day, x_sel, preferred_element_type=jnp.float32)).astype(jnp.bfloat16)
    inv_g = inv_day.reshape(groups, BW, BW).astype(jnp.float32)
    solved = jnp.einsum('gij,gj->gi', inv_g, resid.reshape(groups, BW).astype(jnp.float32)).reshape(L)
    gfull = jnp.einsum('gij,gjm->gim', inv_g, coup_day.reshape(groups, BW, M).astype(jnp.float32)).reshape(L, M)
    gmat = (gfull * colmask[None, :]).astype(jnp.bfloat16)
    qrows = jnp.take(q_cols, index, axis=0)
    qsub = jnp.take(qrows, index, axis=1)
    hmat = jnp.dot(gmat, qsub, preferred_element_type=jnp.float32)
    diag_inv = jnp.diagonal(inv_g, axis1=1, axis2=2).reshape(L)
    cov = diag_inv + jnp.sum(hmat * gmat.astype(jnp.float32), axis=1)
    return solved, cov


def reference(stations, counts, q_cols, glob_solution, inv_blocks, coupling, local_rhs):
    solved, cov = lax.map(lambda inputs: one_day(q_cols, glob_solution, inputs),
                          (stations, counts, inv_blocks, coupling, local_rhs))
    return solved, cov
```

```python
import functools

import jax
import jax.numpy as jnp
from jax import lax
from jax.experimental import pallas as pl
from jax.experimental.pallas import tpu as pltpu
from jax.sharding import PartitionSpec as P

MESH = pl.DeviceIdType.MESH


def pack_kernel(dims, st_ref, q_ref, items_ref, pos_ref, xpos_ref, seen_ref):
    nd, nc, cap, kmax, day_dev, offs, width = dims
    slots = day_dev * kmax
    days_at = lax.axis_index("days")
    me = days_at * nc + lax.axis_index("cols")

    def clear(b, carry):
        seen_ref[b] = 0
        return carry

    lax.fori_loop(0, nd * nc, clear, 0)

    def place(s, carry):
        owner = st_ref[days_at * slots + s]
        rank = seen_ref[owner]
        seen_ref[owner] = rank + 1
        pos_ref[s] = owner * cap + rank
        xpos_ref[s] = lax.rem(owner, nc) * nd + lax.div(owner, nc)
        return carry

    lax.fori_loop(0, slots, place, 0)

    def dest(e, carry):
        def search(s, state):
            count, found = state
            hit = st_ref[e * slots + s] == me
            found = tuple(
                jnp.where(jnp.logical_and(hit, count == i), s, f) for i, f in enumerate(found)
            )
            return count + hit.astype(jnp.int32), found

        zero = jnp.int32(0)
        _, found = lax.fori_loop(0, slots, search, (zero, (zero,) * cap), unroll=8)
        for i, f in enumerate(found):
            k = lax.rem(f, kmax)
            base = e * slots + f - k
            for j in range(offs):
                block = q_ref[st_ref[base + lax.rem(k + j, kmax)]]
                if 0 < j < offs - 1:
                    block = block + block
                items_ref[e, i, j * width : (j + 1) * width, :] = block
        return carry

    lax.fori_loop(0, nd, dest, 0)


def main_kernel(
    dims,
    pos_ref,
    xpos_ref,
    counts_ref,
    x_ref,
    rhs_ref,
    items_ref,
    inv_ref,
    coup_ref,
    solved_ref,
    cov_ref,
    pool,
    xs,
    gm,
    acc,
    sol_rows,
    cov_rows,
    cbuf,
    ibuf,
    csem,
    isem,
    lsem,
    xs1,
    xr1,
    xs2,
    xr2,
    s1,
    r1,
    s2,
    r2,
    s3,
    r3,
):
    nd, nc, cap, kmax, day_dev, offs, width = dims
    rows = acc.shape[0]
    groups = rows // width
    me_d = lax.axis_index("days")
    me_c = lax.axis_index("cols")
    far_c = lax.rem(me_c + nc // 2, nc)
    near_c = me_c + 1 - 2 * lax.rem(me_c, 2)

    def fetch(d, slot):
        return (
            pltpu.make_async_copy(coup_ref.at[d], cbuf.at[slot], csem.at[slot]),
            pltpu.make_async_copy(inv_ref.at[d], ibuf.at[slot], isem.at[slot]),
        )

    for copy in fetch(0, 0):
        copy.start()

    def day_of(r):
        return lax.rem(me_d + r, nd)

    def source_of(r):
        return lax.rem(me_d + nd - r, nd)

    barrier = pltpu.get_barrier_semaphore()

    def greet(r, carry):
        pl.semaphore_signal(barrier, inc=1, device_id=(day_of(r), me_c), device_id_type=MESH)
        return carry

    lax.fori_loop(1, nd, greet, 0)
    for other in (far_c, near_c):
        pl.semaphore_signal(barrier, inc=1, device_id=(me_d, other), device_id_type=MESH)

    def pool_of(d, c):
        return pool.at[pl.ds((d * nc + c) * cap, cap)]

    own_item = pltpu.make_async_copy(items_ref.at[me_d], pool_of(me_d, me_c), lsem.at[0])
    own_item.start()
    own_x = pltpu.make_async_copy(x_ref, xs.at[me_c * nd + me_d], lsem.at[1])
    own_x.start()
    pl.semaphore_wait(barrier, nd + 1)

    def x_first(r, landing):
        return pltpu.make_async_remote_copy(
            src_ref=x_ref,
            dst_ref=xs.at[me_c * nd + landing],
            send_sem=xs1.at[r],
            recv_sem=xr1.at[r],
            device_id=(day_of(r), me_c),
            device_id_type=MESH,
        )

    def x_pass(c, to, at):
        return pltpu.make_async_remote_copy(
            src_ref=xs.at[pl.ds(c * nd, nd)],
            dst_ref=xs.at[pl.ds(c * nd, nd)],
            send_sem=xs2.at[at],
            recv_sem=xr2.at[at],
            device_id=(me_d, to),
            device_id_type=MESH,
        )

    def first(r, landing):
        return pltpu.make_async_remote_copy(
            src_ref=items_ref.at[day_of(r)],
            dst_ref=pool_of(landing, me_c),
            send_sem=s1.at[r],
            recv_sem=r1.at[r],
            device_id=(day_of(r), me_c),
            device_id_type=MESH,
        )

    def across(r, c):
        return pltpu.make_async_remote_copy(
            src_ref=pool_of(source_of(r), c),
            dst_ref=pool_of(source_of(r), c),
            send_sem=s2.at[r],
            recv_sem=r2.at[r],
            device_id=(me_d, far_c),
            device_id_type=MESH,
        )

    def beside(r, c, at):
        return pltpu.make_async_remote_copy(
            src_ref=pool_of(source_of(r), c),
            dst_ref=pool_of(source_of(r), c),
            send_sem=s3.at[at, r],
            recv_sem=r3.at[at, r],
            device_id=(me_d, near_c),
            device_id_type=MESH,
        )

    def send_all(r, carry):
        x_first(r, me_d).start()
        return carry

    lax.fori_loop(1, nd, send_all, 0)

    def send_items(r, carry):
        first(r, me_d).start()
        return carry

    lax.fori_loop(1, nd, send_items, 0)
    own_item.wait()
    across(0, me_c).start()
    beside(0, me_c, 0).start()

    own_x.wait()

    def take_x(r, carry):
        x_first(r, source_of(r)).wait_recv()
        return carry

    lax.fori_loop(1, nd, take_x, 0)
    x_pass(me_c, far_c, 0).start()
    x_pass(me_c, near_c, 1).start()
    x_pass(far_c, far_c, 0).wait_recv()
    x_pass(far_c, near_c, 2).start()
    x_pass(near_c, near_c, 1).wait_recv()
    far_near = near_c + far_c - me_c
    x_pass(far_near, near_c, 2).wait_recv()

    def pass_on(r):
        first(r, source_of(r)).wait_recv()
        across(r, me_c).start()
        beside(r, me_c, 0).start()

    def relay(r):
        across(r, far_c).wait_recv()
        beside(r, far_c, 1).start()

    nt = (((1,), (1,)), ((), ()))
    per_day = -(-nd // day_dev)
    eye = lax.broadcasted_iota(jnp.int32, (width, width), 0) == lax.broadcasted_iota(
        jnp.int32, (width, width), 1
    )

    def day(d, carry):
        slot = lax.rem(d, 2)

        @pl.when(d + 1 < day_dev)
        def _():
            for copy in fetch(d + 1, 1 - slot):
                copy.start()

        for copy in fetch(d, slot):
            copy.wait()
        count = counts_ref[me_d * day_dev + d]
        on = [jnp.where(k < count, 1.0, 0.0).astype(jnp.float32) for k in range(kmax)]
        x8 = jnp.concatenate([xs[xpos_ref[d * kmax + k]] * on[k] for k in range(kmax)], axis=1)
        prod = lax.dot_general(
            x8.astype(jnp.bfloat16), cbuf[slot], nt, preferred_element_type=jnp.float32
        )
        resid = (rhs_ref[pl.ds(d, 1), :] - prod).astype(jnp.bfloat16)
        for g in range(groups):
            part = slice(g * width, (g + 1) * width)
            block = ibuf[slot, part, :]
            solved = lax.dot_general(
                resid[:, part], block, nt, preferred_element_type=jnp.float32
            )
            sol_rows[d, :, part] = solved[:1]
            diag = jnp.sum(jnp.where(eye, block.astype(jnp.float32), 0.0), axis=0, keepdims=True)
            cov_rows[d, :, part] = diag
            full = jnp.dot(block, cbuf[slot, part, :], preferred_element_type=jnp.float32)
            for k in range(kmax):
                gm[d, k, part, :] = (full[:, k * width : (k + 1) * width] * on[k]).astype(
                    jnp.bfloat16
                )

        def step(i, inner):
            r = d * per_day + i

            @pl.when(jnp.logical_and(r > 0, r < nd))
            def _():
                pass_on(r)
                relay(r - 1)

            return inner

        lax.fori_loop(0, per_day, step, 0)
        return carry

    lax.fori_loop(0, day_dev, day, 0)
    relay(nd - 1)

    def finish(r, carry):
        @pl.when(r > 0)
        def _():
            x_first(r, me_d).wait_send()
            first(r, me_d).wait_send()

        across(r, me_c).wait_send()
        beside(r, me_c, 0).wait_send()
        beside(r, far_c, 1).wait_send()
        beside(r, near_c, 0).wait_recv()
        beside(r, far_near, 1).wait_recv()
        return carry

    lax.fori_loop(0, nd, finish, 0)
    x_pass(me_c, far_c, 0).wait_send()
    x_pass(me_c, near_c, 1).wait_send()
    x_pass(far_c, near_c, 2).wait_send()

    pad = jnp.zeros((width, width), jnp.bfloat16)

    def quad(d, carry):
        for k in range(0, kmax, 2):
            left = jnp.concatenate([gm[d, (k + i) % kmax] for i in range(offs + 1)], axis=1)
            one = jnp.concatenate([pool[pos_ref[d * kmax + k]], pad], axis=0)
            two = jnp.concatenate([pad, pool[pos_ref[d * kmax + k + 1]]], axis=0)
            right = jnp.concatenate([one, two], axis=1)
            prod = jnp.dot(left, right, preferred_element_type=jnp.float32)
            term = prod[:, :width] * gm[d, k].astype(jnp.float32) + prod[:, width:] * gm[
                d, k + 1
            ].astype(jnp.float32)
            if k == 0:
                acc[...] = term
            else:
                acc[...] += term
        for g in range(groups):
            part = slice(g * width, (g + 1) * width)
            cov_rows[d, :, part] += jnp.sum(acc[part, :].T, axis=0, keepdims=True)
        return carry

    lax.fori_loop(0, day_dev, quad, 0)
    for d in range(day_dev):
        solved_ref[d : d + 1, :] = sol_rows[d]
        cov_ref[d : d + 1, :] = cov_rows[d]


def local(stations, counts, q_cols, glob_solution, inv_blocks, coupling, local_rhs):
    nd = lax.axis_size("days")
    nc = lax.axis_size("cols")
    day_dev, rows, width = inv_blocks.shape
    kmax = stations.shape[1]
    span = kmax * width
    nblocks = nd * nc
    cap = (day_dev * kmax + nblocks - 1) // nblocks
    offs = kmax // 2 + 1
    slots = day_dev * kmax
    dims = (nd, nc, cap, kmax, day_dev, offs, width)
    tiles = q_cols.reshape(q_cols.shape[0] // width, width, width)
    smem = pl.BlockSpec(memory_space=pltpu.SMEM)
    vmem = pl.BlockSpec(memory_space=pltpu.VMEM)
    hbm = pl.BlockSpec(memory_space=pl.ANY)
    items, pos, xpos = pl.pallas_call(
        functools.partial(pack_kernel, dims),
        out_shape=(
            jax.ShapeDtypeStruct((nd, cap, offs * width, width), jnp.bfloat16),
            jax.ShapeDtypeStruct((slots,), jnp.int32),
            jax.ShapeDtypeStruct((slots,), jnp.int32),
        ),
        in_specs=[smem, vmem],
        out_specs=(vmem, smem, smem),
        scratch_shapes=[pltpu.SMEM((nblocks,), jnp.int32)],
        name="pack",
    )(stations.reshape(-1), tiles)
    x_own = jnp.broadcast_to(glob_solution[None, :], (8, width))
    dma = pltpu.SemaphoreType.DMA
    solved, cov = pl.pallas_call(
        functools.partial(main_kernel, dims),
        out_shape=(
            jax.ShapeDtypeStruct((day_dev, rows), jnp.float32),
            jax.ShapeDtypeStruct((day_dev, rows), jnp.float32),
        ),
        in_specs=[smem, smem, smem, vmem, vmem, hbm, hbm, hbm],
        out_specs=(vmem, vmem),
        scratch_shapes=[
            pltpu.VMEM((nblocks * cap, offs * width, width), jnp.bfloat16),
            pltpu.VMEM((nblocks, 8, width), jnp.float32),
            pltpu.VMEM((day_dev, kmax, rows, width), jnp.bfloat16),
            pltpu.VMEM((rows, width), jnp.float32),
            pltpu.VMEM((day_dev, 1, rows), jnp.float32),
            pltpu.VMEM((day_dev, 1, rows), jnp.float32),
            pltpu.VMEM((2, rows, span), jnp.bfloat16),
            pltpu.VMEM((2, rows, width), jnp.bfloat16),
            dma((2,)),
            dma((2,)),
            dma((2,)),
            dma((nd,)),
            dma((nd,)),
            dma((3,)),
            dma((3,)),
            dma((nd,)),
            dma((nd,)),
            dma((nd,)),
            dma((nd,)),
            dma((2, nd)),
            dma((2, nd)),
        ],
        compiler_params=pltpu.CompilerParams(
            collective_id=0, has_side_effects=True, vmem_limit_bytes=62 * 1024 * 1024
        ),
        name="solve",
    )(pos, xpos, counts, x_own, local_rhs, items, inv_blocks, coupling)
    return solved, cov


def solution(mesh):
    return jax.shard_map(
        local,
        mesh=mesh,
        in_specs=(
            P(),
            P(),
            P(None, ("days", "cols")),
            P(("days", "cols")),
            P("days", "cols", None),
            P("days", "cols", None),
            P("days", "cols"),
        ),
        out_specs=(P("days", "cols"), P("days", "cols")),
        check_vma=False,
    )
```

```python
import functools

import jax
import jax.numpy as jnp
from jax import lax
from jax.experimental import pallas as pl
from jax.experimental.pallas import tpu as pltpu
from jax.sharding import PartitionSpec as P

MESH = pl.DeviceIdType.MESH


def units_of(cap, kmax):
    per_slot = kmax - 1
    return 2 + cap * per_slot, per_slot


def pack_kernel(dims, st_ref, q_ref, items_ref, pos_ref, dpos_ref, xpos_ref, seen_ref):
    nd, nc, cap, kmax, day_dev, width = dims
    units, per_slot = units_of(cap, kmax)
    half, unit = kmax // 2, width // 2
    slots = day_dev * kmax
    days_at = lax.axis_index("days")
    me = days_at * nc + lax.axis_index("cols")

    def clear(b, carry):
        seen_ref[b] = 0
        return carry

    lax.fori_loop(0, nd * nc, clear, 0)

    def place(s, carry):
        owner = st_ref[days_at * slots + s]
        rank = seen_ref[owner]
        seen_ref[owner] = rank + 1
        pos_ref[s] = owner * units + 2 + rank * per_slot
        dpos_ref[s] = owner * units
        xpos_ref[s] = lax.rem(owner, nc) * nd + lax.div(owner, nc)
        return carry

    lax.fori_loop(0, slots, place, 0)

    def dest(e, carry):
        def search(s, state):
            count, found = state
            hit = st_ref[e * slots + s] == me
            found = tuple(
                jnp.where(jnp.logical_and(hit, count == i), s, f) for i, f in enumerate(found)
            )
            return count + hit.astype(jnp.int32), found

        zero = jnp.int32(0)
        _, found = lax.fori_loop(0, slots, search, (zero, (zero,) * cap), unroll=8)
        own = q_ref[me]
        items_ref[e, 0] = own[:unit]
        items_ref[e, 1] = own[unit:]
        for i, f in enumerate(found):
            k = lax.rem(f, kmax)
            base = e * slots + f - k
            at = 2 + i * per_slot
            for j in range(1, half):
                block = q_ref[st_ref[base + lax.rem(k + j, kmax)]]
                block = block + block
                items_ref[e, at + 2 * j - 2] = block[:unit]
                items_ref[e, at + 2 * j - 1] = block[unit:]
            block = q_ref[st_ref[base + lax.rem(k + half, kmax)]]
            block = block + block
            items_ref[e, at + per_slot - 1] = jnp.where(k < half, block[:unit], block.T[unit:])
        return carry

    lax.fori_loop(0, nd, dest, 0)


def main_kernel(
    dims,
    pos_ref,
    dpos_ref,
    xpos_ref,
    counts_ref,
    x_ref,
    rhs_ref,
    items_ref,
    inv_ref,
    coup_ref,
    solved_ref,
    cov_ref,
    pool,
    xs,
    gm,
    acc,
    sol_rows,
    cov_rows,
    cbuf,
    ibuf,
    csem,
    isem,
    lsem,
    xs1,
    xr1,
    xs2,
    xr2,
    s1,
    r1,
    s2,
    r2,
    s3,
    r3,
):
    nd, nc, cap, kmax, day_dev, width = dims
    units, per_slot = units_of(cap, kmax)
    half = kmax // 2
    rows = acc.shape[0]
    groups = rows // width
    me_d = lax.axis_index("days")
    me_c = lax.axis_index("cols")
    far_c = lax.rem(me_c + nc // 2, nc)
    near_c = me_c + 1 - 2 * lax.rem(me_c, 2)

    def fetch(d, slot):
        return (
            pltpu.make_async_copy(coup_ref.at[d], cbuf.at[slot], csem.at[slot]),
            pltpu.make_async_copy(inv_ref.at[d], ibuf.at[slot], isem.at[slot]),
        )

    for copy in fetch(0, 0):
        copy.start()

    def day_of(r):
        peer, bit = 0, 1
        while bit < nd:
            peer = peer + lax.rem(me_d // bit + r // bit, 2) * bit
            bit *= 2
        return peer

    source_of = day_of

    barrier = pltpu.get_barrier_semaphore()

    def greet(r, carry):
        pl.semaphore_signal(barrier, inc=1, device_id=(day_of(r), me_c), device_id_type=MESH)
        return carry

    lax.fori_loop(1, nd, greet, 0)
    for other in (far_c, near_c):
        pl.semaphore_signal(barrier, inc=1, device_id=(me_d, other), device_id_type=MESH)

    def pool_of(d, c):
        return pool.at[pl.ds((d * nc + c) * units, units)]

    own_item = pltpu.make_async_copy(items_ref.at[me_d], pool_of(me_d, me_c), lsem.at[0])
    own_item.start()
    own_x = pltpu.make_async_copy(x_ref, xs.at[me_c * nd + me_d], lsem.at[1])
    own_x.start()
    pl.semaphore_wait(barrier, nd + 1)

    def x_first(r, landing):
        return pltpu.make_async_remote_copy(
            src_ref=x_ref,
            dst_ref=xs.at[me_c * nd + landing],
            send_sem=xs1.at[r],
            recv_sem=xr1.at[r],
            device_id=(day_of(r), me_c),
            device_id_type=MESH,
        )

    def x_pass(c, to, at):
        return pltpu.make_async_remote_copy(
            src_ref=xs.at[pl.ds(c * nd, nd)],
            dst_ref=xs.at[pl.ds(c * nd, nd)],
            send_sem=xs2.at[at],
            recv_sem=xr2.at[at],
            device_id=(me_d, to),
            device_id_type=MESH,
        )

    def first(r, landing):
        return pltpu.make_async_remote_copy(
            src_ref=items_ref.at[day_of(r)],
            dst_ref=pool_of(landing, me_c),
            send_sem=s1.at[r],
            recv_sem=r1.at[r],
            device_id=(day_of(r), me_c),
            device_id_type=MESH,
        )

    def across(r, c):
        return pltpu.make_async_remote_copy(
            src_ref=pool_of(source_of(r), c),
            dst_ref=pool_of(source_of(r), c),
            send_sem=s2.at[r],
            recv_sem=r2.at[r],
            device_id=(me_d, far_c),
            device_id_type=MESH,
        )

    def beside(r, c, at):
        return pltpu.make_async_remote_copy(
            src_ref=pool_of(source_of(r), c),
            dst_ref=pool_of(source_of(r), c),
            send_sem=s3.at[at, r],
            recv_sem=r3.at[at, r],
            device_id=(me_d, near_c),
            device_id_type=MESH,
        )

    def send_all(r, carry):
        x_first(r, me_d).start()
        return carry

    lax.fori_loop(1, nd, send_all, 0)

    def send_items(r, carry):
        first(r, me_d).start()
        return carry

    lax.fori_loop(1, nd, send_items, 0)
    own_item.wait()
    across(0, me_c).start()
    beside(0, me_c, 0).start()

    own_x.wait()

    def take_x(r, carry):
        x_first(r, source_of(r)).wait_recv()
        return carry

    lax.fori_loop(1, nd, take_x, 0)
    x_pass(me_c, far_c, 0).start()
    x_pass(me_c, near_c, 1).start()
    x_pass(far_c, far_c, 0).wait_recv()
    x_pass(far_c, near_c, 2).start()
    x_pass(near_c, near_c, 1).wait_recv()
    far_near = near_c + far_c - me_c
    x_pass(far_near, near_c, 2).wait_recv()

    def pass_on(r):
        first(r, source_of(r)).wait_recv()
        across(r, me_c).start()
        beside(r, me_c, 0).start()

    def relay(r):
        across(r, far_c).wait_recv()
        beside(r, far_c, 1).start()

    nt = (((1,), (1,)), ((), ()))
    per_day = -(-nd // day_dev)
    eye = lax.broadcasted_iota(jnp.int32, (width, width), 0) == lax.broadcasted_iota(
        jnp.int32, (width, width), 1
    )

    def day(d, carry):
        slot = lax.rem(d, 2)

        @pl.when(d + 1 < day_dev)
        def _():
            for copy in fetch(d + 1, 1 - slot):
                copy.start()

        for copy in fetch(d, slot):
            copy.wait()
        count = counts_ref[me_d * day_dev + d]
        on = [jnp.where(k < count, 1.0, 0.0).astype(jnp.float32) for k in range(kmax)]
        x8 = jnp.concatenate([xs[xpos_ref[d * kmax + k]] * on[k] for k in range(kmax)], axis=1)
        prod = lax.dot_general(
            x8.astype(jnp.bfloat16), cbuf[slot], nt, preferred_element_type=jnp.float32
        )
        resid = (rhs_ref[pl.ds(d, 1), :] - prod).astype(jnp.bfloat16)
        for g in range(groups):
            part = slice(g * width, (g + 1) * width)
            block = ibuf[slot, part, :]
            solved = lax.dot_general(
                resid[:, part], block, nt, preferred_element_type=jnp.float32
            )
            sol_rows[d, :, part] = solved[:1]
            diag = jnp.sum(jnp.where(eye, block.astype(jnp.float32), 0.0), axis=0, keepdims=True)
            cov_rows[d, :, part] = diag
            full = jnp.dot(block, cbuf[slot, part, :], preferred_element_type=jnp.float32)
            for k in range(kmax):
                gm[d, k, part, :] = (full[:, k * width : (k + 1) * width] * on[k]).astype(
                    jnp.bfloat16
                )

        def step(i, inner):
            r = d * per_day + i

            @pl.when(jnp.logical_and(r > 0, r < nd))
            def _():
                pass_on(r)
                relay(r - 1)

            return inner

        lax.fori_loop(0, per_day, step, 0)
        return carry

    lax.fori_loop(0, day_dev, day, 0)
    relay(nd - 1)

    def finish(r, carry):
        @pl.when(r > 0)
        def _():
            x_first(r, me_d).wait_send()
            first(r, me_d).wait_send()

        across(r, me_c).wait_send()
        beside(r, me_c, 0).wait_send()
        beside(r, far_c, 1).wait_send()
        beside(r, near_c, 0).wait_recv()
        beside(r, far_near, 1).wait_recv()
        return carry

    lax.fori_loop(0, nd, finish, 0)
    x_pass(me_c, far_c, 0).wait_send()
    x_pass(me_c, near_c, 1).wait_send()
    x_pass(far_c, near_c, 2).wait_send()

    pad = jnp.zeros((width, width), jnp.bfloat16)

    def column(d, k):
        mine, diag = pos_ref[d * kmax + k], dpos_ref[d * kmax + k]
        parts = [pool[diag], pool[diag + 1]]
        parts += [pool[mine + i] for i in range(per_slot - 1)]
        if k < half:
            mate = pos_ref[d * kmax + k + half]
            parts += [pool[mine + per_slot - 1], pool[mate + per_slot - 1]]
        return jnp.concatenate(parts, axis=0)

    def quad(d, carry):
        for k in range(0, kmax, 2):
            count = half + 2 if k < half else half + 1
            left = jnp.concatenate([gm[d, (k + i) % kmax] for i in range(count)], axis=1)
            one = jnp.concatenate([column(d, k), pad], axis=0)
            two = jnp.concatenate([pad, column(d, k + 1)], axis=0)
            right = jnp.concatenate([one, two], axis=1)
            prod = jnp.dot(left, right, preferred_element_type=jnp.float32)
            term = prod[:, :width] * gm[d, k].astype(jnp.float32) + prod[:, width:] * gm[
                d, k + 1
            ].astype(jnp.float32)
            if k == 0:
                acc[...] = term
            else:
                acc[...] += term
        for g in range(groups):
            part = slice(g * width, (g + 1) * width)
            cov_rows[d, :, part] += jnp.sum(acc[part, :].T, axis=0, keepdims=True)
        return carry

    lax.fori_loop(0, day_dev, quad, 0)
    for d in range(day_dev):
        solved_ref[d : d + 1, :] = sol_rows[d]
        cov_ref[d : d + 1, :] = cov_rows[d]


def local(stations, counts, q_cols, glob_solution, inv_blocks, coupling, local_rhs):
    nd = lax.axis_size("days")
    nc = lax.axis_size("cols")
    day_dev, rows, width = inv_blocks.shape
    kmax = stations.shape[1]
    span = kmax * width
    nblocks = nd * nc
    cap = (day_dev * kmax + nblocks - 1) // nblocks
    units, _ = units_of(cap, kmax)
    slots = day_dev * kmax
    dims = (nd, nc, cap, kmax, day_dev, width)
    tiles = q_cols.reshape(q_cols.shape[0] // width, width, width)
    smem = pl.BlockSpec(memory_space=pltpu.SMEM)
    vmem = pl.BlockSpec(memory_space=pltpu.VMEM)
    hbm = pl.BlockSpec(memory_space=pl.ANY)
    items, pos, dpos, xpos = pl.pallas_call(
        functools.partial(pack_kernel, dims),
        out_shape=(
            jax.ShapeDtypeStruct((nd, units, width // 2, width), jnp.bfloat16),
            jax.ShapeDtypeStruct((slots,), jnp.int32),
            jax.ShapeDtypeStruct((slots,), jnp.int32),
            jax.ShapeDtypeStruct((slots,), jnp.int32),
        ),
        in_specs=[smem, vmem],
        out_specs=(vmem, smem, smem, smem),
        scratch_shapes=[pltpu.SMEM((nblocks,), jnp.int32)],
        name="pack",
    )(stations.reshape(-1), tiles)
    x_own = jnp.broadcast_to(glob_solution[None, :], (8, width))
    dma = pltpu.SemaphoreType.DMA
    solved, cov = pl.pallas_call(
        functools.partial(main_kernel, dims),
        out_shape=(
            jax.ShapeDtypeStruct((day_dev, rows), jnp.float32),
            jax.ShapeDtypeStruct((day_dev, rows), jnp.float32),
        ),
        in_specs=[smem, smem, smem, smem, vmem, vmem, hbm, hbm, hbm],
        out_specs=(vmem, vmem),
        scratch_shapes=[
            pltpu.VMEM((nblocks * units, width // 2, width), jnp.bfloat16),
            pltpu.VMEM((nblocks, 8, width), jnp.float32),
            pltpu.VMEM((day_dev, kmax, rows, width), jnp.bfloat16),
            pltpu.VMEM((rows, width), jnp.float32),
            pltpu.VMEM((day_dev, 1, rows), jnp.float32),
            pltpu.VMEM((day_dev, 1, rows), jnp.float32),
            pltpu.VMEM((2, rows, span), jnp.bfloat16),
            pltpu.VMEM((2, rows, width), jnp.bfloat16),
            dma((2,)),
            dma((2,)),
            dma((2,)),
            dma((nd,)),
            dma((nd,)),
            dma((3,)),
            dma((3,)),
            dma((nd,)),
            dma((nd,)),
            dma((nd,)),
            dma((nd,)),
            dma((2, nd)),
            dma((2, nd)),
        ],
        compiler_params=pltpu.CompilerParams(
            collective_id=0, has_side_effects=True, vmem_limit_bytes=62 * 1024 * 1024
        ),
        name="solve",
    )(pos, dpos, xpos, counts, x_own, local_rhs, items, inv_blocks, coupling)
    return solved, cov


def solution(mesh):
    return jax.shard_map(
        local,
        mesh=mesh,
        in_specs=(
            P(),
            P(),
            P(None, ("days", "cols")),
            P(("days", "cols")),
            P("days", "cols", None),
            P("days", "cols", None),
            P("days", "cols"),
        ),
        out_specs=(P("days", "cols"), P("days", "cols")),
        check_vma=False,
    )
```

```python
import functools

import jax
import jax.numpy as jnp
from jax import lax
from jax.experimental import pallas as pl
from jax.experimental.pallas import tpu as pltpu
from jax.sharding import PartitionSpec as P

MESH = pl.DeviceIdType.MESH


def units_of(cap, kmax):
    per_slot = kmax - 1
    return 2 + cap * per_slot, per_slot


def pack_kernel(dims, st_ref, q_ref, items_ref, pos_ref, dpos_ref, xpos_ref, seen_ref):
    nd, nc, cap, kmax, day_dev, width = dims
    units, per_slot = units_of(cap, kmax)
    half, unit = kmax // 2, width // 2
    slots = day_dev * kmax
    days_at = lax.axis_index("days")
    me = days_at * nc + lax.axis_index("cols")

    def clear(b, carry):
        seen_ref[b] = 0
        return carry

    lax.fori_loop(0, nd * nc, clear, 0)

    def place(s, carry):
        owner = st_ref[days_at * slots + s]
        rank = seen_ref[owner]
        seen_ref[owner] = rank + 1
        pos_ref[s] = owner * units + 2 + rank * per_slot
        dpos_ref[s] = owner * units
        xpos_ref[s] = lax.rem(owner, nc) * nd + lax.div(owner, nc)
        return carry

    lax.fori_loop(0, slots, place, 0)

    def dest(e, carry):
        def search(s, state):
            count, found = state
            hit = st_ref[e * slots + s] == me
            found = tuple(
                jnp.where(jnp.logical_and(hit, count == i), s, f) for i, f in enumerate(found)
            )
            return count + hit.astype(jnp.int32), found

        zero = jnp.int32(0)
        _, found = lax.fori_loop(0, slots, search, (zero, (zero,) * cap), unroll=8)
        own = q_ref[me]
        items_ref[e, 0] = own[:unit]
        items_ref[e, 1] = own[unit:]
        for i, f in enumerate(found):
            k = lax.rem(f, kmax)
            base = e * slots + f - k
            at = 2 + i * per_slot
            for j in range(1, half):
                block = q_ref[st_ref[base + lax.rem(k + j, kmax)]]
                block = block + block
                items_ref[e, at + 2 * j - 2] = block[:unit]
                items_ref[e, at + 2 * j - 1] = block[unit:]
            block = q_ref[st_ref[base + lax.rem(k + half, kmax)]]
            block = block + block
            items_ref[e, at + per_slot - 1] = jnp.where(k < half, block[:unit], block.T[unit:])
        return carry

    lax.fori_loop(0, nd, dest, 0)


def main_kernel(
    dims,
    pos_ref,
    dpos_ref,
    xpos_ref,
    counts_ref,
    x_ref,
    rhs_ref,
    items_ref,
    inv_ref,
    coup_ref,
    solved_ref,
    cov_ref,
    pool,
    xs,
    gm,
    acc,
    sol_rows,
    cov_rows,
    cbuf,
    ibuf,
    csem,
    isem,
    lsem,
    xs1,
    xr1,
    xs2,
    xr2,
    s1,
    r1,
    s2,
    r2,
    s3,
    r3,
):
    nd, nc, cap, kmax, day_dev, width = dims
    units, per_slot = units_of(cap, kmax)
    half = kmax // 2
    rows = acc.shape[0]
    groups = rows // width
    me_d = lax.axis_index("days")
    me_c = lax.axis_index("cols")
    far_c = lax.rem(me_c + nc // 2, nc)
    near_c = me_c + 1 - 2 * lax.rem(me_c, 2)

    def fetch(d, slot):
        return (
            pltpu.make_async_copy(coup_ref.at[d], cbuf.at[slot], csem.at[slot]),
            pltpu.make_async_copy(inv_ref.at[d], ibuf.at[slot], isem.at[slot]),
        )

    for copy in fetch(0, 0):
        copy.start()

    def day_of(r):
        peer, bit = 0, 1
        while bit < nd:
            peer = peer + lax.rem(me_d // bit + r // bit, 2) * bit
            bit *= 2
        return peer

    source_of = day_of

    barrier = pltpu.get_barrier_semaphore()

    def greet(r, carry):
        pl.semaphore_signal(barrier, inc=1, device_id=(day_of(r), me_c), device_id_type=MESH)
        return carry

    lax.fori_loop(1, nd, greet, 0)
    for other in (far_c, near_c):
        pl.semaphore_signal(barrier, inc=1, device_id=(me_d, other), device_id_type=MESH)

    def pool_of(d, c):
        return pool.at[pl.ds((d * nc + c) * units, units)]

    own_item = pltpu.make_async_copy(items_ref.at[me_d], pool_of(me_d, me_c), lsem.at[0])
    own_item.start()
    own_x = pltpu.make_async_copy(x_ref, xs.at[me_c * nd + me_d], lsem.at[1])
    own_x.start()
    pl.semaphore_wait(barrier, nd + 1)

    def x_first(r, landing):
        return pltpu.make_async_remote_copy(
            src_ref=x_ref,
            dst_ref=xs.at[me_c * nd + landing],
            send_sem=xs1.at[r],
            recv_sem=xr1.at[r],
            device_id=(day_of(r), me_c),
            device_id_type=MESH,
        )

    def x_pass(c, to, at):
        return pltpu.make_async_remote_copy(
            src_ref=xs.at[pl.ds(c * nd, nd)],
            dst_ref=xs.at[pl.ds(c * nd, nd)],
            send_sem=xs2.at[at],
            recv_sem=xr2.at[at],
            device_id=(me_d, to),
            device_id_type=MESH,
        )

    def first(r, landing):
        return pltpu.make_async_remote_copy(
            src_ref=items_ref.at[day_of(r)],
            dst_ref=pool_of(landing, me_c),
            send_sem=s1.at[r],
            recv_sem=r1.at[r],
            device_id=(day_of(r), me_c),
            device_id_type=MESH,
        )

    def across(r, c):
        return pltpu.make_async_remote_copy(
            src_ref=pool_of(source_of(r), c),
            dst_ref=pool_of(source_of(r), c),
            send_sem=s2.at[r],
            recv_sem=r2.at[r],
            device_id=(me_d, far_c),
            device_id_type=MESH,
        )

    def beside(r, c, at):
        return pltpu.make_async_remote_copy(
            src_ref=pool_of(source_of(r), c),
            dst_ref=pool_of(source_of(r), c),
            send_sem=s3.at[at, r],
            recv_sem=r3.at[at, r],
            device_id=(me_d, near_c),
            device_id_type=MESH,
        )

    def send_all(r, carry):
        x_first(r, me_d).start()
        return carry

    lax.fori_loop(1, nd, send_all, 0)

    def send_items(r, carry):
        first(r, me_d).start()
        return carry

    lax.fori_loop(1, nd, send_items, 0)
    own_item.wait()
    across(0, me_c).start()
    beside(0, me_c, 0).start()

    own_x.wait()

    def take_x(r, carry):
        x_first(r, source_of(r)).wait_recv()
        return carry

    lax.fori_loop(1, nd, take_x, 0)
    x_pass(me_c, far_c, 0).start()
    x_pass(me_c, near_c, 1).start()
    x_pass(far_c, far_c, 0).wait_recv()
    x_pass(far_c, near_c, 2).start()
    x_pass(near_c, near_c, 1).wait_recv()
    far_near = near_c + far_c - me_c
    x_pass(far_near, near_c, 2).wait_recv()

    def pass_on(r):
        first(r, source_of(r)).wait_recv()
        across(r, me_c).start()
        beside(r, me_c, 0).start()

    def relay(r):
        across(r, far_c).wait_recv()
        beside(r, far_c, 1).start()

    nt = (((1,), (1,)), ((), ()))
    per_day = -(-nd // day_dev)
    eye = lax.broadcasted_iota(jnp.int32, (width, width), 0) == lax.broadcasted_iota(
        jnp.int32, (width, width), 1
    )

    def day(d, carry):
        slot = lax.rem(d, 2)

        @pl.when(d + 1 < day_dev)
        def _():
            for copy in fetch(d + 1, 1 - slot):
                copy.start()

        for copy in fetch(d, slot):
            copy.wait()
        count = counts_ref[me_d * day_dev + d]
        on = [jnp.where(k < count, 1.0, 0.0).astype(jnp.float32) for k in range(kmax)]
        x8 = jnp.concatenate([xs[xpos_ref[d * kmax + k]] * on[k] for k in range(kmax)], axis=1)
        prod = lax.dot_general(
            x8.astype(jnp.bfloat16), cbuf[slot], nt, preferred_element_type=jnp.float32
        )
        resid = (rhs_ref[pl.ds(d, 1), :] - prod).astype(jnp.bfloat16)
        for g in range(groups):
            part = slice(g * width, (g + 1) * width)
            block = ibuf[slot, part, :]
            solved = lax.dot_general(
                resid[:, part], block, nt, preferred_element_type=jnp.float32
            )
            sol_rows[d, :, part] = solved[:1]
            diag = jnp.sum(jnp.where(eye, block.astype(jnp.float32), 0.0), axis=0, keepdims=True)
            cov_rows[d, :, part] = diag
            full = jnp.dot(block, cbuf[slot, part, :], preferred_element_type=jnp.float32)
            for k in range(kmax):
                gm[d, k, part, :] = (full[:, k * width : (k + 1) * width] * on[k]).astype(
                    jnp.bfloat16
                )

        def step(i, inner):
            r = d * per_day + i

            @pl.when(jnp.logical_and(r > 0, r < nd))
            def _():
                pass_on(r)
                relay(r - 1)

            return inner

        lax.fori_loop(0, per_day, step, 0)
        return carry

    lax.fori_loop(0, day_dev, day, 0)
    relay(nd - 1)

    def arrive(r, carry):
        beside(r, near_c, 0).wait_recv()
        beside(r, far_near, 1).wait_recv()
        return carry

    lax.fori_loop(0, nd, arrive, 0)

    pad = jnp.zeros((width, width), jnp.bfloat16)

    def column(d, k):
        mine, diag = pos_ref[d * kmax + k], dpos_ref[d * kmax + k]
        parts = [pool[diag], pool[diag + 1]]
        parts += [pool[mine + i] for i in range(per_slot - 1)]
        if k < half:
            mate = pos_ref[d * kmax + k + half]
            parts += [pool[mine + per_slot - 1], pool[mate + per_slot - 1]]
        return jnp.concatenate(parts, axis=0)

    def quad(d, carry):
        for k in range(0, kmax, 2):
            count = half + 2 if k < half else half + 1
            left = jnp.concatenate([gm[d, (k + i) % kmax] for i in range(count)], axis=1)
            one = jnp.concatenate([column(d, k), pad], axis=0)
            two = jnp.concatenate([pad, column(d, k + 1)], axis=0)
            right = jnp.concatenate([one, two], axis=1)
            prod = jnp.dot(left, right, preferred_element_type=jnp.float32)
            term = prod[:, :width] * gm[d, k].astype(jnp.float32) + prod[:, width:] * gm[
                d, k + 1
            ].astype(jnp.float32)
            if k == 0:
                acc[...] = term
            else:
                acc[...] += term
        for g in range(groups):
            part = slice(g * width, (g + 1) * width)
            cov_rows[d, :, part] += jnp.sum(acc[part, :].T, axis=0, keepdims=True)
        return carry

    lax.fori_loop(0, day_dev, quad, 0)

    def sent(r, carry):
        @pl.when(r > 0)
        def _():
            x_first(r, me_d).wait_send()
            first(r, me_d).wait_send()

        across(r, me_c).wait_send()
        beside(r, me_c, 0).wait_send()
        beside(r, far_c, 1).wait_send()
        return carry

    lax.fori_loop(0, nd, sent, 0)
    x_pass(me_c, far_c, 0).wait_send()
    x_pass(me_c, near_c, 1).wait_send()
    x_pass(far_c, near_c, 2).wait_send()
    for d in range(day_dev):
        solved_ref[d : d + 1, :] = sol_rows[d]
        cov_ref[d : d + 1, :] = cov_rows[d]


def local(stations, counts, q_cols, glob_solution, inv_blocks, coupling, local_rhs):
    nd = lax.axis_size("days")
    nc = lax.axis_size("cols")
    day_dev, rows, width = inv_blocks.shape
    kmax = stations.shape[1]
    span = kmax * width
    nblocks = nd * nc
    cap = (day_dev * kmax + nblocks - 1) // nblocks
    units, _ = units_of(cap, kmax)
    slots = day_dev * kmax
    dims = (nd, nc, cap, kmax, day_dev, width)
    tiles = q_cols.reshape(q_cols.shape[0] // width, width, width)
    smem = pl.BlockSpec(memory_space=pltpu.SMEM)
    vmem = pl.BlockSpec(memory_space=pltpu.VMEM)
    hbm = pl.BlockSpec(memory_space=pl.ANY)
    items, pos, dpos, xpos = pl.pallas_call(
        functools.partial(pack_kernel, dims),
        out_shape=(
            jax.ShapeDtypeStruct((nd, units, width // 2, width), jnp.bfloat16),
            jax.ShapeDtypeStruct((slots,), jnp.int32),
            jax.ShapeDtypeStruct((slots,), jnp.int32),
            jax.ShapeDtypeStruct((slots,), jnp.int32),
        ),
        in_specs=[smem, vmem],
        out_specs=(vmem, smem, smem, smem),
        scratch_shapes=[pltpu.SMEM((nblocks,), jnp.int32)],
        name="pack",
    )(stations.reshape(-1), tiles)
    x_own = jnp.broadcast_to(glob_solution[None, :], (8, width))
    dma = pltpu.SemaphoreType.DMA
    solved, cov = pl.pallas_call(
        functools.partial(main_kernel, dims),
        out_shape=(
            jax.ShapeDtypeStruct((day_dev, rows), jnp.float32),
            jax.ShapeDtypeStruct((day_dev, rows), jnp.float32),
        ),
        in_specs=[smem, smem, smem, smem, vmem, vmem, hbm, hbm, hbm],
        out_specs=(vmem, vmem),
        scratch_shapes=[
            pltpu.VMEM((nblocks * units, width // 2, width), jnp.bfloat16),
            pltpu.VMEM((nblocks, 8, width), jnp.float32),
            pltpu.VMEM((day_dev, kmax, rows, width), jnp.bfloat16),
            pltpu.VMEM((rows, width), jnp.float32),
            pltpu.VMEM((day_dev, 1, rows), jnp.float32),
            pltpu.VMEM((day_dev, 1, rows), jnp.float32),
            pltpu.VMEM((2, rows, span), jnp.bfloat16),
            pltpu.VMEM((2, rows, width), jnp.bfloat16),
            dma((2,)),
            dma((2,)),
            dma((2,)),
            dma((nd,)),
            dma((nd,)),
            dma((3,)),
            dma((3,)),
            dma((nd,)),
            dma((nd,)),
            dma((nd,)),
            dma((nd,)),
            dma((2, nd)),
            dma((2, nd)),
        ],
        compiler_params=pltpu.CompilerParams(
            collective_id=0, has_side_effects=True, vmem_limit_bytes=62 * 1024 * 1024
        ),
        name="solve",
    )(pos, dpos, xpos, counts, x_own, local_rhs, items, inv_blocks, coupling)
    return solved, cov


def solution(mesh):
    return jax.shard_map(
        local,
        mesh=mesh,
        in_specs=(
            P(),
            P(),
            P(None, ("days", "cols")),
            P(("days", "cols")),
            P("days", "cols", None),
            P("days", "cols", None),
            P("days", "cols"),
        ),
        out_specs=(P("days", "cols"), P("days", "cols")),
        check_vma=False,
    )
```
